256 devices in a mesh: slab: 16 (over z_hi, x, core), space: 16 (over z_lo, y).
Axes of the slice: x: 4, y: 4, z: 8 (z_hi: 2, z_lo: 4; z = z_hi * 4 + z_lo), core: 2. Of those that a mesh axis runs over, the one named last changes fastest.
Arguments:
- state_old: float32 [16, 3, 32, 128, 128], P('slab', None, 'space'), may hold values from -6 to 6
- coarse_old: float32 [16, 3, 32, 128, 128], P('slab', None, 'space'), may hold values from -6 to 6
- source: float32 [16, 3, 32, 128, 128], P('slab', None, 'space'), may hold values from -3 to 3
- start_state: float32 [3, 32, 128, 128], P(None, 'space'), may hold values from -6 to 6
- conduct: float32 [32, 128, 128], P('space'), may hold values from 0.05 to 1
- reluct: float32 [32, 128, 128], P('space'), may hold values from 0.25 to 1
- converged: int32 [1], replicated, may hold values from 0 to 16383
Outputs:
- state_new: float32 [16, 3, 32, 128, 128], P('slab', None, 'space')
- coarse_new: float32 [16, 3, 32, 128, 128], P('slab', None, 'space')
The draws below stay inside these ranges and needn't reach their ends.
Inputs may be any that keep to these rules, and one draw needn't show every extreme that they name: converged mod 16 names the slab group that has converged.
All inputs are finite; a program needn't handle non-finite values.
Results may differ from the reference program's by a relative error of at most 0.0003.
Values sent between devices are 32-bit elements; how exact they have to be, the bound alone decides.
No kernel may reach another device: no remote copies, remote signals or barrier semaphores. Data moves between devices by JAX's collectives and lax.ppermute only.
A program may use at most 64 MiB of HBM per device.

```python
import math
import jax
import jax.numpy as jnp
from jax import lax

NY = 128
NZ = 128
FSTEPS = 2
FSWEEPS = 8
CSWEEPS = 2
SLABS = 16
NX = 32


def levels(key, extent, pieces, low, top_value):
    def one(dim, blocks):
        steps = jax.random.uniform(jax.random.fold_in(jax.random.fold_in(key, 6), dim), (blocks,), jnp.float32, low / len(pieces), top_value / len(pieces))
        return jnp.repeat(jnp.exp(steps), extent[dim] // blocks).reshape((-1,) + (1,) * (len(extent) - dim - 1))

    gain = one(*pieces[0])
    for cut in pieces[1:]:
        gain = gain * one(*cut)
    return gain


def gaussian(stream_key, shape, scale, limit, pieces=(), held_as=jnp.bfloat16):
    values = jax.random.normal(stream_key, shape, jnp.float32) * scale
    if len(pieces) > 0:
        values = levels(stream_key, shape, pieces, -0.22, 0.18) * values
    return jnp.clip(values, min=-limit, max=limit).astype(held_as)


def setup_inputs(seed: int = 0) -> dict:
    streams_of = jax.random.split(jax.random.key(seed), 8)
    state_old = gaussian(streams_of[0], (SLABS, 3, NX, NY, NZ), 1.0, 6.0, ((0, 16), (2, 16)), jnp.float32)
    coarse_old = gaussian(streams_of[1], (SLABS, 3, NX, NY, NZ), 1.0, 6.0, ((0, 16), (2, 16)), jnp.float32)
    source = gaussian(streams_of[2], (SLABS, 3, NX, NY, NZ), 0.5, 3.0, ((0, 16), (2, 16)), jnp.float32)
    start_state = gaussian(streams_of[3], (3, NX, NY, NZ), 1.0, 6.0, ((1, 16),), jnp.float32)
    conduct = jnp.clip(jnp.exp(math.log(1.0) - 2.9957323 * jax.random.uniform(streams_of[4], (NX, NY, NZ), jnp.float32) ** levels(streams_of[4], (NX, NY, NZ), ((0, 16),), -0.2, 0.2)), 0.05, 1.0)
    reluct = jnp.clip(jnp.exp(math.log(1.0) - 1.3862944 * jax.random.uniform(streams_of[5], (NX, NY, NZ), jnp.float32) ** levels(streams_of[5], (NX, NY, NZ), ((0, 16),), -0.2, 0.2)), 0.25, 1.0)
    converged = jax.random.randint(streams_of[6], (1,), 0, SLABS * 1024).astype(jnp.int32)
    return {"state_old": state_old, "coarse_old": coarse_old, "source": source, "start_state": start_state, "conduct": conduct, "reluct": reluct, "converged": converged}


floor_rate = 0.05
top_rate = 1.0
curl_bound = 14.0


def forward(array, along, border):
    interior = lax.slice_in_dim(array, 1, array.shape[along], axis=along)
    return jnp.concatenate((interior, border), along) - array


def backward(array, along, border):
    interior = lax.slice_in_dim(array, 0, array.shape[along] - 1, axis=along)
    return jnp.concatenate((border, interior), along) - array


def zero_plane(array, along):
    return jnp.zeros_like(lax.slice_in_dim(array, 0, 1, axis=along))


def operate(edge_field, mass_term, reluct):
    x_part, y_part, z_part = edge_field[0], edge_field[1], edge_field[2]
    curl_x = reluct * (forward(z_part, 1, zero_plane(z_part, 1)) - forward(y_part, 2, zero_plane(y_part, 2)))
    curl_y = reluct * (forward(x_part, 2, zero_plane(x_part, 2)) - forward(z_part, 0, zero_plane(z_part, 0)))
    curl_z = reluct * (forward(y_part, 0, zero_plane(y_part, 0)) - forward(x_part, 1, zero_plane(x_part, 1)))
    k_x = backward(curl_y, 2, zero_plane(curl_y, 2)) - backward(curl_z, 1, zero_plane(curl_z, 1))
    k_y = backward(curl_z, 0, zero_plane(curl_z, 0)) - backward(curl_x, 2, zero_plane(curl_x, 2))
    k_z = backward(curl_x, 1, zero_plane(curl_x, 1)) - backward(curl_y, 0, zero_plane(curl_y, 0))
    return mass_term * edge_field + jnp.stack((k_x, k_y, k_z))


def chebyshev(target, initial, mass_term, reluct, lower_bound, upper_bound, sweeps):
    center = 0.5 * (upper_bound + lower_bound)
    radius = 0.5 * (upper_bound - lower_bound)
    spread = center / radius
    rho_now = 1.0 / spread
    residual = target - operate(initial, mass_term, reluct)
    iterate = initial
    update = residual / center
    for repeat in range(sweeps):
        iterate = iterate + update
        if repeat + 1 < sweeps:
            residual = residual - operate(update, mass_term, reluct)
            rho_next = 1.0 / (2.0 * spread - rho_now)
            update = (rho_next * rho_now) * update + (2.0 * rho_next / radius) * residual
            rho_now = rho_next
    return iterate


def reference(state_old, coarse_old, source, start_state, conduct, reluct, converged):
    fine_mass = FSTEPS * conduct
    fine_floor = FSTEPS * floor_rate
    fine_top = FSTEPS * top_rate + curl_bound
    coarse_top = top_rate + curl_bound

    def fine_run(inputs):
        iterate, slab_source = inputs
        for repeat in range(FSTEPS):
            iterate = chebyshev(fine_mass * iterate + slab_source, iterate, fine_mass, reluct, fine_floor, fine_top, FSWEEPS)
        return iterate

    fine_end = lax.map(fine_run, (state_old, source))
    offset = (converged[0] % SLABS + 1) % SLABS

    def advance(incoming, position):
        slab_index = ((offset + position) % SLABS).astype(jnp.int32)
        slab_source = lax.dynamic_index_in_dim(source, slab_index, 0, keepdims=False)
        coarse = chebyshev(conduct * incoming + slab_source, incoming, conduct, reluct, floor_rate, coarse_top, CSWEEPS)
        fine_slab = lax.dynamic_index_in_dim(fine_end, slab_index, 0, keepdims=False)
        old_slab = lax.dynamic_index_in_dim(coarse_old, slab_index, 0, keepdims=False)
        outgoing = coarse + (fine_slab - old_slab)
        return outgoing, (incoming, coarse)

    finish, outputs = lax.scan(advance, start_state, jnp.arange(SLABS, dtype=jnp.int32))
    states, coarses = outputs
    return jnp.roll(states, offset, axis=0), jnp.roll(coarses, offset, axis=0)
```

```python
import functools

import jax
import jax.numpy as jnp
from jax import lax
from jax.experimental import pallas as pl
from jax.experimental.pallas import tpu as pltpu
from jax.sharding import PartitionSpec as P

FSTEPS = 2
FSWEEPS = 8
CSWEEPS = 2

floor_rate = 0.05
top_rate = 1.0
curl_bound = 14.0

ROWS = 8


def chebyshev_weights(lower, upper, sweeps):
    theta, delta = 0.5 * (upper + lower), 0.5 * (upper - lower)
    sigma = theta / delta
    top = [1.0, sigma]
    for _ in range(sweeps):
        top.append(2.0 * sigma * top[-1] - top[-2])
    step = [1.0 / theta] + [0.0] * (sweeps - 1)
    weights = list(step)
    rho = 1.0 / sigma
    for k in range(1, sweeps):
        rho_next = 1.0 / (2.0 * sigma - rho)
        step = [rho_next * rho * v for v in step]
        step[k] += 2.0 * rho_next / delta / top[k]
        weights = [a + b for a, b in zip(weights, step)]
        rho = rho_next
    return theta, delta, weights, top[sweeps]


FINE = chebyshev_weights(FSTEPS * floor_rate, FSTEPS * top_rate + curl_bound, FSWEEPS)
COARSE = chebyshev_weights(floor_rate, top_rate + curl_bound, CSWEEPS)


def shifts(shape):
    rows, lanes = shape
    lane = lax.broadcasted_iota(jnp.int32, shape, 1)
    not_last, not_first = lane < lanes - 1, lane > 0

    def next_z(v):
        return jnp.where(not_last, pltpu.roll(v, lanes - 1, axis=1), 0.0)

    def prev_z(v):
        return jnp.where(not_first, pltpu.roll(v, 1, axis=1), 0.0)

    def next_y(v):
        return pltpu.roll(v, rows - 1, axis=0)

    def prev_y(v):
        return pltpu.roll(v, 1, axis=0)

    return next_z, prev_z, next_y, prev_y


def curl_sweep(field, rel, keep_top, emit, planes):
    rows = field.shape[2]
    next_z, prev_z, next_y, prev_y = shifts((rows, 128))

    def prev_y_in(v):
        w = prev_y(v)
        return jnp.concatenate((w[: rows - ROWS], w[rows - ROWS :] * keep_top), 0)

    def body(i, carry):
        hy_low, hz_low = carry
        ex, ey, ez = field[i, 0], field[i, 1], field[i, 2]
        ey_up, ez_up = field[i + 1, 1], field[i + 1, 2]
        nu = rel[i]
        hx = nu * ((next_y(ez) - ez) - (next_z(ey) - ey))
        hy = nu * ((next_z(ex) - ex) - (ez_up - ez))
        hz = nu * ((ey_up - ey) - (next_y(ex) - ex))
        kx = (prev_z(hy) - hy) - (prev_y_in(hz) - hz)
        ky = (hz_low - hz) - (prev_z(hx) - hx)
        kz = (prev_y_in(hx) - hx) - (hy_low - hy)
        emit(i, (ex, ey, ez), (kx, ky, kz))
        return hy, hz

    zero = jnp.zeros((rows, 128), jnp.float32)
    lax.fori_loop(0, planes, body, (zero, zero), unroll=2)


def load_rows(dst, low, own, high, blocks):
    def body(b, _):
        for j in range(2):
            for comp in range(3):
                dst[2 * b + j, comp, 0:ROWS] = low[b, comp, j]
                dst[2 * b + j, comp, ROWS : 2 * ROWS] = own[b, comp, j]
                dst[2 * b + j, comp, 2 * ROWS : 3 * ROWS] = high[b, comp, j]
        return 0

    lax.fori_loop(0, blocks, body, 0)
    for comp in range(3):
        dst[2 * blocks, comp] = jnp.zeros((3 * ROWS, 128), jnp.float32)


MID = slice(ROWS, 2 * ROWS)


def fine_kernel(first, flags, low, own, high, con, rel, *rest):
    if first:
        total, after, here, there, quot, nu2 = rest
    else:
        other, base, out, here, there, quot, nu2, total = rest
    blocks = own.shape[0]
    planes = 2 * blocks
    theta, delta, weights, scale = FINE
    keep_top = flags[0]
    load_rows(here, low, own, high, blocks)
    for comp in range(3):
        there[planes, comp] = jnp.zeros((3 * ROWS, 128), jnp.float32)

    def prepare(i, _):
        quot[i] = 2.0 * theta / delta - (2.0 * FSTEPS / delta) * con[i]
        nu2[i] = (2.0 / delta) * rel[i]
        return 0

    lax.fori_loop(0, planes, prepare, 0)

    buffers = (here, there)
    last = FSWEEPS if first else FSWEEPS - 1
    for k in range(last):
        now, new = buffers[k % 2], buffers[(k + 1) % 2]

        def emit(i, e, curl, k=k, new=new):
            b, j = i // 2, i % 2
            q = quot[i]
            for comp in range(3):
                v = q * e[comp] - curl[comp]
                if k == 0:
                    v = 0.5 * v
                    new[i, comp] = v
                    total[b, comp, j] = weights[0] * e[comp][MID] + weights[1] * v[MID]
                    continue
                if k + 1 < FSWEEPS:
                    v = v - new[i, comp]
                    new[i, comp] = v
                    acc = total[b, comp, j] + weights[k + 1] * v[MID]
                    if k + 1 == FSWEEPS - 1 and not first:
                        acc = base[b, comp, j] + flags[1] * (acc + other[b, comp, j])
                        out[b, comp, j] = acc
                    else:
                        total[b, comp, j] = acc
                else:
                    v = v[MID] - new[i, comp, MID]
                    mass = FSTEPS * con[i, MID]
                    after[b, comp, j] = (1.0 / scale) * v + mass * total[b, comp, j]

        curl_sweep(now, nu2, keep_top, emit, planes)


def coarse_kernel(count, flags, low, own, high, con, rel, out, state, curled, fac, nu3):
    blocks = own.shape[0]
    planes = 2 * blocks
    theta, delta, weights, _ = COARSE
    keep_top = flags[0]
    load_rows(state, low, own, high, blocks)
    for comp in range(3):
        curled[planes, comp] = jnp.zeros((3 * ROWS, 128), jnp.float32)

    def prepare(i, _):
        fac[i] = (weights[0] + weights[1] * theta / delta) - (weights[1] / delta) * con[i]
        nu3[i] = (weights[1] / delta) * rel[i]
        return 0

    lax.fori_loop(0, planes, prepare, 0)

    def one(final):
        def first(i, e, curl):
            for comp in range(3):
                curled[i, comp] = curl[comp]

        curl_sweep(state, rel, keep_top, first, planes)

        def second(i, u, curl):
            f = fac[i]
            for comp in range(3):
                v = state[i, comp] - f * u[comp] + curl[comp]
                if final:
                    out[i // 2, comp, i % 2] = v[MID]
                else:
                    state[i, comp] = v

        curl_sweep(curled, nu3, keep_top, second, planes)

    if count > 1:
        lax.fori_loop(0, count - 1, lambda n, z: (one(False), z)[1], 0)
    one(True)


def start_kernel(flags, state, old, src, begin, con, rel, state_up, state_low, src_up, src_low, rel_low, res, base, forced):
    planes = con.shape[0]
    ny = con.shape[1]
    theta, delta, weights, _ = COARSE
    next_z, prev_z, next_y, prev_y = shifts((ny, 128))
    row = lax.broadcasted_iota(jnp.int32, (ny, 128), 0)
    raw_next, raw_prev = next_y, prev_y

    def next_y(v):
        return jnp.where(row < ny - 1, raw_next(v), 0.0)

    def prev_y(v):
        return jnp.where(row > 0, raw_prev(v), 0.0)

    def curls(field, up, low):
        nu = rel_low[0]
        ex, ey, ez = low[0], low[1], low[2]
        hy_low = nu * ((next_z(ex) - ex) - (field[2, 0] - ez))
        hz_low = nu * ((field[1, 0] - ey) - (next_y(ex) - ex))
        for i in range(planes):
            ex, ey, ez = field[0, i], field[1, i], field[2, i]
            ey_up = field[1, i + 1] if i + 1 < planes else up[0]
            ez_up = field[2, i + 1] if i + 1 < planes else up[1]
            nu = rel[i]
            hx = nu * ((next_y(ez) - ez) - (next_z(ey) - ey))
            hy = nu * ((next_z(ex) - ex) - (ez_up - ez))
            hz = nu * ((ey_up - ey) - (next_y(ex) - ex))
            kx = (prev_z(hy) - hy) - (prev_y(hz) - hz)
            ky = (hz_low - hz) - (prev_z(hx) - hx)
            kz = (prev_y(hx) - hx) - (hy_low - hy)
            yield i, (ex, ey, ez), (kx, ky, kz)
            hy_low, hz_low = hy, hz

    def spread(ref, comp, i, v):
        for b in range(ny // ROWS):
            ref[b, comp, i] = v[b * ROWS : (b + 1) * ROWS]

    for i, e, curl in curls(state, state_up, state_low):
        for comp in range(3):
            spread(res, comp, i, src[comp, i] - curl[comp])
    for i, s, curl in curls(src, src_up, src_low):
        fac = (weights[0] + weights[1] * theta / delta) - (weights[1] / delta) * con[i]
        for comp in range(3):
            push = fac * s[comp] - (weights[1] / delta) * curl[comp]
            forced[comp, i] = push
            inner = state[comp, i] - old[comp, i] + push
            spread(base, comp, i, jnp.where(flags[1] > 0.0, inner, begin[comp, i]))


VMEM = pl.BlockSpec(memory_space=pltpu.VMEM)
SMEM = pl.BlockSpec(memory_space=pltpu.SMEM)


def call(kernel, name, outs, scratch, flags, *operands):
    return pl.pallas_call(
        kernel,
        name=name,
        out_shape=[jax.ShapeDtypeStruct(s, jnp.float32) for s in outs],
        in_specs=[SMEM] + [VMEM] * len(operands),
        out_specs=[VMEM] * len(outs),
        scratch_shapes=[pltpu.VMEM(s, jnp.float32) for s in scratch],
    )(flags, *operands)


def open_shift(value, steps):
    count = lax.axis_size("space")
    first, last = max(0, -steps), min(count, count - steps)
    return lax.ppermute(value, "space", [(i, i + steps) for i in range(first, last)])


def ring_shift(value, steps):
    count = lax.axis_size("slab")
    return lax.ppermute(value, "slab", [(i, (i + steps) % count) for i in range(count)])


def turn(value):
    return lax.all_to_all(value, "space", 0, 0, tiled=True)


def halo(value):
    return open_shift(value, 1), open_shift(value, -1)


def local(state_old, coarse_old, source, start_state, conduct, reluct, converged):
    groups = lax.axis_size("slab")
    spaces = lax.axis_size("space")
    position = (lax.axis_index("slab") - converged[0] % groups - 1) % groups
    turnpos = (position + 1) % groups
    inner = lax.axis_index("space") < spaces - 1
    flags = jnp.stack((inner, turnpos > 0)).astype(jnp.float32)
    state, src = state_old[0], source[0]
    planes, ny = conduct.shape[0], conduct.shape[1]
    blocks = spaces
    field = (blocks, 3, planes, ROWS, 128)
    nx = blocks * planes

    ups = open_shift(jnp.stack((state[1:3, 0], src[1:3, 0])), -1)
    lows = open_shift(jnp.concatenate((state[:, -1], src[:, -1], reluct[-1:])), 1)
    coef = jnp.stack((conduct, reluct)).reshape(2, planes, blocks, ROWS, 128).transpose(2, 0, 1, 3, 4)
    coef = turn(coef)
    coef_low, coef_high = halo(coef)
    coef24 = jnp.concatenate((coef_low, coef, coef_high), 3).transpose(1, 0, 2, 3, 4).reshape(2, nx, 3 * ROWS, 128)
    con, rel = coef24[0], coef24[1]

    res, base, forced = call(
        start_kernel, "start", [field, field, state.shape], [], flags,
        state, coarse_old[0], src, start_state, conduct, reluct,
        ups[0], lows[0:3], ups[1], lows[3:6], lows[6:7],
    )
    res = turn(res)
    res_low, res_high = halo(res)
    base = turn(base)

    wide = (nx + 1, 3, 3 * ROWS, 128)
    slim = (nx, 3 * ROWS, 128)
    total, after = call(
        functools.partial(fine_kernel, True), "fine_first", [field, field], [wide, wide, slim, slim], flags,
        res_low, res, res_high, con, rel,
    )
    after_low, after_high = halo(after)
    (lead,) = call(
        functools.partial(fine_kernel, False), "fine_second", [field], [wide, wide, slim, slim, field], flags,
        after_low, after, after_high, con, rel, total, base,
    )

    def coarse(value, count):
        low, high = halo(value)
        return call(
            functools.partial(coarse_kernel, count), "coarse%d" % count, [field], [wide, wide, slim, slim], flags,
            low, value, high, con, rel,
        )[0]

    def masked(value, condition):
        return jnp.where(condition, value, 0.0)

    lead = lead + masked(ring_shift(coarse(lead, 1), 1), turnpos >= 1)
    lead = lead + masked(ring_shift(coarse(lead, 2), 2), turnpos >= 2)
    chained = ring_shift(lead, 1)
    power = lead
    for step in range(4, groups, 4):
        power = coarse(power, 4)
        chained = chained + masked(ring_shift(power, step + 1), position >= step)
    moved = coarse(chained, 1)

    def home(value):
        return turn(value).transpose(1, 2, 0, 3, 4).reshape(3, planes, ny, 128)

    return home(chained)[None], (home(moved) + forced)[None]


def solution(mesh):
    placed = (
        P("slab", None, "space", None, None),
        P("slab", None, "space", None, None),
        P("slab", None, "space", None, None),
        P(None, "space", None, None),
        P("space", None, None),
        P("space", None, None),
        P(),
    )
    return jax.shard_map(
        local,
        mesh=mesh,
        in_specs=placed,
        out_specs=(P("slab", None, "space", None, None), P("slab", None, "space", None, None)),
        check_vma=False,
    )
```

```python
import functools

import jax
import jax.numpy as jnp
from jax import lax
from jax.experimental import pallas as pl
from jax.experimental.pallas import tpu as pltpu
from jax.sharding import PartitionSpec as P

FSTEPS = 2
FSWEEPS = 8
CSWEEPS = 2

floor_rate = 0.05
top_rate = 1.0
curl_bound = 14.0

ROWS = 8
UNROLL = 8


def chebyshev_weights(lower, upper, sweeps):
    theta, delta = 0.5 * (upper + lower), 0.5 * (upper - lower)
    sigma = theta / delta
    top = [1.0, sigma]
    for _ in range(sweeps):
        top.append(2.0 * sigma * top[-1] - top[-2])
    step = [1.0 / theta] + [0.0] * (sweeps - 1)
    weights = list(step)
    rho = 1.0 / sigma
    for k in range(1, sweeps):
        rho_next = 1.0 / (2.0 * sigma - rho)
        step = [rho_next * rho * v for v in step]
        step[k] += 2.0 * rho_next / delta / top[k]
        weights = [a + b for a, b in zip(weights, step)]
        rho = rho_next
    return theta, delta, weights, top[sweeps]


FINE = chebyshev_weights(FSTEPS * floor_rate, FSTEPS * top_rate + curl_bound, FSWEEPS)
COARSE = chebyshev_weights(floor_rate, top_rate + curl_bound, CSWEEPS)


def shifts(shape):
    rows, lanes = shape
    lane = lax.broadcasted_iota(jnp.int32, shape, 1)
    not_last, not_first = lane < lanes - 1, lane > 0

    def next_z(v):
        return jnp.where(not_last, pltpu.roll(v, lanes - 1, axis=1), 0.0)

    def prev_z(v):
        return jnp.where(not_first, pltpu.roll(v, 1, axis=1), 0.0)

    def next_y(v):
        return pltpu.roll(v, rows - 1, axis=0)

    def prev_y(v):
        return pltpu.roll(v, 1, axis=0)

    return next_z, prev_z, next_y, prev_y


def window(margin):
    if margin >= ROWS // 2:
        return 0, 3 * ROWS
    if margin > 0:
        return ROWS // 2, 2 * ROWS
    return 0, 2 * ROWS


def curl_sweep(field, rel, keep_top, margin, emit, planes):
    low, count = window(margin)
    high = low + count
    next_z, prev_z, _, prev_y = shifts((count, 128))
    tail = lax.broadcasted_iota(jnp.int32, (ROWS, 128), 0) + (high - ROWS)
    tail = jnp.where(tail < 2 * ROWS, 1.0, keep_top)
    rows = pl.ds(low, count) if margin else pl.ds(ROWS, ROWS)

    def prev_y_in(v):
        w = prev_y(v)
        if margin:
            w = jnp.concatenate((w[: count - ROWS], w[count - ROWS :] * tail), 0)
        return w

    def crop(v):
        return v if margin else v[ROWS:]

    def body(m, carry):
        hy_low, hz_low = carry
        for j in range(UNROLL):
            i = m * UNROLL + j
            ex, ey, ez = [field[i, comp, low:high] for comp in range(3)]
            ey_up, ez_up = [field[i + 1, comp, low:high] for comp in (1, 2)]
            ex_next, ez_next = [field[i, comp, low + 1 : high + 1] for comp in (0, 2)]
            nu = rel[i, low:high]
            hx = nu * ((ez_next - ez) - (next_z(ey) - ey))
            hy = nu * ((next_z(ex) - ex) - (ez_up - ez))
            hz = nu * ((ey_up - ey) - (ex_next - ex))
            kx = crop(prev_z(hy) - hy) - crop(prev_y_in(hz) - hz)
            ky = crop(hz_low - hz) - crop(prev_z(hx) - hx)
            kz = crop(prev_y_in(hx) - hx) - crop(hy_low - hy)
            emit(i, rows, (kx, ky, kz))
            hy_low, hz_low = hy, hz
        return hy_low, hz_low

    zero = jnp.zeros((count, 128), jnp.float32)
    lax.fori_loop(0, planes // UNROLL, body, (zero, zero))


def load_rows(dst, other, low, own, high, blocks):
    zero = jnp.zeros((ROWS, 128), jnp.float32)
    edge = low.shape[3]

    def body(b, _):
        for j in range(2):
            for comp in range(3):
                i = 2 * b + j
                if edge < ROWS:
                    dst[i, comp, 0:ROWS] = zero
                    dst[i, comp, 2 * ROWS : 3 * ROWS] = zero
                dst[i, comp, ROWS - edge : ROWS] = low[b, comp, j]
                dst[i, comp, ROWS : 2 * ROWS] = own[b, comp, j]
                dst[i, comp, 2 * ROWS : 2 * ROWS + edge] = high[b, comp, j]
                dst[i, comp, 3 * ROWS : 4 * ROWS] = zero
                other[i, comp, 3 * ROWS : 4 * ROWS] = zero
        return 0

    lax.fori_loop(0, blocks, body, 0)
    for comp in range(3):
        dst[2 * blocks, comp] = jnp.zeros((4 * ROWS, 128), jnp.float32)
        other[2 * blocks, comp] = jnp.zeros((4 * ROWS, 128), jnp.float32)


MID = pl.ds(ROWS, ROWS)


def fine_kernel(first, flags, low, own, high, con, rel, *rest):
    if first:
        total, after, here, there, quot, nu2 = rest
    else:
        other, base, out, total, here, there, quot, nu2 = rest
    blocks = own.shape[0]
    planes = 2 * blocks
    theta, delta, weights, scale = FINE
    load_rows(here, there, low, own, high, blocks)

    def prepare(i, _):
        quot[i] = 2.0 * theta / delta - (2.0 * FSTEPS / delta) * con[i]
        nu2[i] = (2.0 / delta) * rel[i]
        return 0

    lax.fori_loop(0, planes, prepare, 0)

    buffers = (here, there)
    sweeps = FSWEEPS if first else FSWEEPS - 1
    for k in range(sweeps):
        now, new = buffers[k % 2], buffers[(k + 1) % 2]

        def emit(i, rows, curl, k=k, now=now, new=new):
            b, j = i // 2, i % 2
            q = quot[i, rows]
            for comp in range(3):
                v = q * now[i, comp, rows] - curl[comp]
                v = 0.5 * v if k == 0 else v - new[i, comp, rows]
                acc = weights[k] * now[i, comp, MID]
                if k > 0:
                    acc = total[b, comp, j] + acc
                elif not first:
                    acc = other[b, comp, j] + acc
                if k + 1 < sweeps:
                    new[i, comp, rows] = v
                elif first:
                    after[b, comp, j] = (1.0 / scale) * v + (FSTEPS * con[i, MID]) * acc
                else:
                    acc = acc + weights[k + 1] * v
                    out[b, comp, j] = base[b, comp, j] + acc
                total[b, comp, j] = acc

        curl_sweep(now, nu2, flags[0], sweeps - 1 - k, emit, planes)


def coarse_kernel(count, gate, flags, low, own, high, con, rel, *rest):
    if gate is None:
        out, state, curled, fac, nu3 = rest
    else:
        extra, out, state, curled, fac, nu3 = rest
    blocks = own.shape[0]
    planes = 2 * blocks
    theta, delta, weights, _ = COARSE
    load_rows(state, curled, low, own, high, blocks)

    def prepare(i, _):
        fac[i] = (weights[0] + weights[1] * theta / delta) - (weights[1] / delta) * con[i]
        nu3[i] = (weights[1] / delta) * rel[i]
        return 0

    lax.fori_loop(0, planes, prepare, 0)

    for n in range(count):
        margin = 2 * (count - 1 - n)

        def first(i, rows, curl):
            for comp in range(3):
                curled[i, comp, rows] = curl[comp]

        curl_sweep(state, rel, flags[0], margin + 1, first, planes)

        def second(i, rows, curl, margin=margin):
            f = fac[i, rows]
            for comp in range(3):
                v = state[i, comp, rows] - f * curled[i, comp, rows] + curl[comp]
                if margin:
                    state[i, comp, rows] = v
                elif gate is None:
                    out[i // 2, comp, i % 2] = v
                else:
                    out[i // 2, comp, i % 2] = extra[i // 2, comp, i % 2] + jnp.where(flags[gate] > 0.0, v, 0.0)

        curl_sweep(curled, nu3, flags[0], margin, second, planes)


def plane_curls(ny):
    next_z, prev_z, raw_next, raw_prev = shifts((ny, 128))
    row = lax.broadcasted_iota(jnp.int32, (ny, 128), 0)

    def next_y(v):
        return jnp.where(row < ny - 1, raw_next(v), 0.0)

    def prev_y(v):
        return jnp.where(row > 0, raw_prev(v), 0.0)

    def curl(nu, e, up):
        ex, ey, ez = e
        hx = nu * ((next_y(ez) - ez) - (next_z(ey) - ey))
        hy = nu * ((next_z(ex) - ex) - (up[1] - ez))
        hz = nu * ((up[0] - ey) - (next_y(ex) - ex))
        return hx, hy, hz

    def back(h, low):
        hx, hy, hz = h
        kx = (prev_z(hy) - hy) - (prev_y(hz) - hz)
        ky = (low[2] - hz) - (prev_z(hx) - hx)
        kz = (prev_y(hx) - hx) - (low[1] - hy)
        return kx, ky, kz

    return curl, back


def spread(ref, comp, i, v):
    for b in range(v.shape[0] // ROWS):
        ref[b, comp, i] = v[b * ROWS : (b + 1) * ROWS]


def residual_kernel(flags, state, src, rel, up, low, rel_low, res):
    planes, ny = rel.shape[0], rel.shape[1]
    curl, back = plane_curls(ny)
    before = curl(rel_low[0], (low[0], low[1], low[2]), (state[1, 0], state[2, 0]))
    for i in range(planes):
        nxt = (state[1, i + 1], state[2, i + 1]) if i + 1 < planes else (up[0], up[1])
        here = curl(rel[i], (state[0, i], state[1, i], state[2, i]), nxt)
        k = back(here, before)
        for comp in range(3):
            spread(res, comp, i, src[comp, i] - k[comp])
        before = here


def base_kernel(flags, state, old, src, con, rel, up, low, rel_low, begin, begin_up, begin_low, base, work):
    planes, ny = con.shape[0], con.shape[1]
    theta, delta, weights, _ = COARSE
    curl, back = plane_curls(ny)

    def fac(i):
        return (weights[0] + weights[1] * theta / delta) - (weights[1] / delta) * con[i]

    before = curl(rel_low[0], (low[0], low[1], low[2]), (src[1, 0], src[2, 0]))
    for i in range(planes):
        nxt = (src[1, i + 1], src[2, i + 1]) if i + 1 < planes else (up[0], up[1])
        here = curl(rel[i], (src[0, i], src[1, i], src[2, i]), nxt)
        k = back(here, before)
        for comp in range(3):
            push = fac(i) * src[comp, i] - (weights[1] / delta) * k[comp]
            spread(base, comp, i, state[comp, i] - old[comp, i] + push)
        before = here

    @pl.when(flags[1] > 0.0)
    def _():
        def part(i, comp):
            if i < 0:
                return begin_low[comp * planes + planes + i]
            return begin[comp, i] if i < planes else begin_up[comp * planes + i - planes]

        def nu(i):
            if i < 0:
                return begin_low[3 * planes + planes + i]
            return rel[i] if i < planes else begin_up[3 * planes + i - planes]

        def h_of(i):
            above = (part(i + 1, 1), part(i + 1, 2))
            return curl(nu(i), (part(i, 0), part(i, 1), part(i, 2)), above)

        before = h_of(-2)
        for i in range(-1, planes + 1):
            here = h_of(i)
            k = back(here, before)
            for comp in range(3):
                work[i + 1, comp] = k[comp] * flags[2] if i == planes else k[comp]
            before = here
        before = None
        for i in range(-1, planes):
            u = [work[i + 1, comp] for comp in range(3)]
            here = curl(nu(i), u, (work[i + 2, 1], work[i + 2, 2]))
            if i >= 0:
                k = back(here, before)
                for comp in range(3):
                    v = begin[comp, i] - fac(i) * u[comp] + (weights[1] / delta) * k[comp]
                    for b in range(ny // ROWS):
                        base[b, comp, i] = base[b, comp, i] + v[b * ROWS : (b + 1) * ROWS]
            before = here


VMEM = pl.BlockSpec(memory_space=pltpu.VMEM)
SMEM = pl.BlockSpec(memory_space=pltpu.SMEM)


def call(kernel, name, outs, scratch, flags, *operands):
    return pl.pallas_call(
        kernel,
        name=name,
        out_shape=[jax.ShapeDtypeStruct(s, jnp.float32) for s in outs],
        in_specs=[SMEM] + [VMEM] * len(operands),
        out_specs=[VMEM] * len(outs),
        scratch_shapes=[pltpu.VMEM(s, jnp.float32) for s in scratch],
    )(flags, *operands)


def open_shift(value, steps):
    count = lax.axis_size("space")
    first, last = max(0, -steps), min(count, count - steps)
    return lax.ppermute(value, "space", [(i, i + steps) for i in range(first, last)])


def ring_shift(value, steps):
    count = lax.axis_size("slab")
    return lax.ppermute(value, "slab", [(i, (i + steps) % count) for i in range(count)])


def both_shift(value, steps, along):
    slabs, spaces = lax.axis_size("slab"), lax.axis_size("space")
    pairs = [
        (i * spaces + k, (i + steps) % slabs * spaces + k + along)
        for i in range(slabs)
        for k in range(spaces)
        if 0 <= k + along < spaces
    ]
    return lax.ppermute(value, ("slab", "space"), pairs)


def turn(value):
    return lax.all_to_all(value, "space", 0, 0, tiled=True)


def halo(value):
    return open_shift(value, 1), open_shift(value, -1)


def local(state_old, coarse_old, source, start_state, conduct, reluct, converged):
    groups = lax.axis_size("slab")
    spaces = lax.axis_size("space")
    position = (lax.axis_index("slab") - converged[0] % groups - 1) % groups
    inner = lax.axis_index("space") < spaces - 1
    flags = jnp.stack((inner, position == 0, inner, position >= 1, position >= 2)).astype(jnp.float32)
    state, old, src = state_old[0], coarse_old[0], source[0]
    planes, ny = conduct.shape[0], conduct.shape[1]
    blocks = spaces
    nx = blocks * planes
    field = (blocks, 3, planes, ROWS, 128)

    ups = open_shift(jnp.stack((state[1:3, 0], src[1:3, 0])), -1)
    lows = open_shift(jnp.concatenate((state[:, -1], src[:, -1], reluct[-1:])), 1)
    coef = jnp.stack((conduct, reluct)).reshape(2, planes, blocks, ROWS, 128).transpose(2, 0, 1, 3, 4)
    coef = turn(coef)
    coef_low, coef_high = halo(coef)
    coef24 = jnp.concatenate((coef_low, coef, coef_high), 3).transpose(1, 0, 2, 3, 4).reshape(2, nx, 3 * ROWS, 128)
    con, rel = coef24[0], coef24[1]

    (res,) = call(residual_kernel, "residual", [field], [], flags, state, src, reluct, ups[0], lows[0:3], lows[6:7])
    res = turn(res)
    res_low, res_high = halo(res)

    start_state, res = lax.optimization_barrier((start_state, res))
    edge = jnp.concatenate((start_state.reshape(3 * planes, ny, 128), reluct))
    edge_low, edge_high = halo(edge)

    wide = (nx + 1, 3, 4 * ROWS, 128)
    slim = (nx, 3 * ROWS, 128)
    scratch = [wide, wide, slim, slim]
    total, after = call(
        functools.partial(fine_kernel, True), "fine_first", [field, field], scratch, flags,
        res_low, res, res_high, con, rel,
    )
    after_low, after_high = halo(after)
    src, after = lax.optimization_barrier((src, after))
    (base,) = call(
        base_kernel, "base", [field], [(planes + 2, 3, ny, 128)], flags,
        state, old, src, conduct, reluct, ups[1], lows[3:6], lows[6:7], start_state, edge_high, edge_low,
    )
    base = turn(base)

    lead, total = call(
        functools.partial(fine_kernel, False), "fine_second", [field, field], scratch, flags,
        after_low, after, after_high, con, rel, total, base,
    )

    def coarse(value, count):
        low, high = halo(value)
        return call(
            functools.partial(coarse_kernel, count, None), "coarse%d" % count, [field], scratch, flags,
            low, value, high, con, rel,
        )[0]

    def joined(value, steps, gate):
        rows = 2 * steps
        own = ring_shift(value, steps)
        low = both_shift(value[:, :, :, ROWS - rows :], steps, 1)
        high = both_shift(value[:, :, :, :rows], steps, -1)
        return call(
            functools.partial(coarse_kernel, steps, gate), "joined%d" % steps, [field], scratch, flags,
            low, own, high, con, rel, value,
        )[0]

    lead = joined(lead, 1, 3)
    lead = joined(lead, 2, 4)
    final, power = lead, lead
    for steps in range(4, groups, 4):
        power = coarse(power, 4)
        final = final + jnp.where(position >= steps, ring_shift(power, steps), 0.0)
    starts = ring_shift(final, 1)
    ends = final - total

    def home(value):
        return turn(value).transpose(1, 2, 0, 3, 4).reshape(3, planes, ny, 128)

    coarse_new = home(ends) + (old - state)
    state_new = jnp.where(position == 0, start_state, home(starts))
    return state_new[None], coarse_new[None]


def solution(mesh):
    placed = (
        P("slab", None, "space", None, None),
        P("slab", None, "space", None, None),
        P("slab", None, "space", None, None),
        P(None, "space", None, None),
        P("space", None, None),
        P("space", None, None),
        P(),
    )
    return jax.shard_map(
        local,
        mesh=mesh,
        in_specs=placed,
        out_specs=(P("slab", None, "space", None, None), P("slab", None, "space", None, None)),
        check_vma=False,
    )
```

```python
import functools

import jax
import jax.numpy as jnp
from jax import lax
from jax.experimental import pallas as pl
from jax.experimental.pallas import tpu as pltpu
from jax.sharding import PartitionSpec as P


FSTEPS = 2
FSWEEPS = 8
CSWEEPS = 2

floor_rate = 0.05
top_rate = 1.0
curl_bound = 14.0

ROWS = 8
UNROLL = 8
VMEM_LIMIT = 16 << 20


def chebyshev_weights(lower, upper, sweeps):
    theta, delta = 0.5 * (upper + lower), 0.5 * (upper - lower)
    sigma = theta / delta
    top = [1.0, sigma]
    for _ in range(sweeps):
        top.append(2.0 * sigma * top[-1] - top[-2])
    step = [1.0 / theta] + [0.0] * (sweeps - 1)
    weights = list(step)
    rho = 1.0 / sigma
    for k in range(1, sweeps):
        rho_next = 1.0 / (2.0 * sigma - rho)
        step = [rho_next * rho * v for v in step]
        step[k] += 2.0 * rho_next / delta / top[k]
        weights = [a + b for a, b in zip(weights, step)]
        rho = rho_next
    return theta, delta, weights, top[sweeps]


FINE = chebyshev_weights(FSTEPS * floor_rate, FSTEPS * top_rate + curl_bound, FSWEEPS)
COARSE = chebyshev_weights(floor_rate, top_rate + curl_bound, CSWEEPS)


def shifts(shape):
    rows, lanes = shape
    lane = lax.broadcasted_iota(jnp.int32, shape, 1)
    not_last, not_first = lane < lanes - 1, lane > 0

    def next_z(v):
        return jnp.where(not_last, pltpu.roll(v, lanes - 1, axis=1), 0.0)

    def prev_z(v):
        return jnp.where(not_first, pltpu.roll(v, 1, axis=1), 0.0)

    def next_y(v):
        return pltpu.roll(v, rows - 1, axis=0)

    def prev_y(v):
        return pltpu.roll(v, 1, axis=0)

    return next_z, prev_z, next_y, prev_y


def window(margin):
    if margin >= ROWS // 2:
        return 0, 3 * ROWS
    if margin > 0:
        return ROWS // 2, 2 * ROWS
    return 0, 2 * ROWS


def curl_sweep(field, rel, keep_top, margin, emit, planes):
    low, count = window(margin)
    high = low + count
    next_z, prev_z, _, prev_y = shifts((count, 128))
    tail = lax.broadcasted_iota(jnp.int32, (ROWS, 128), 0) + (high - ROWS)
    tail = jnp.where(tail < 2 * ROWS, 1.0, keep_top)
    rows = pl.ds(low, count) if margin else pl.ds(ROWS, ROWS)

    def prev_y_in(v):
        w = prev_y(v)
        if margin:
            w = jnp.concatenate((w[: count - ROWS], w[count - ROWS :] * tail), 0)
        return w

    def crop(v):
        return v if margin else v[ROWS:]

    def body(m, carry):
        hy_low, hz_low = carry
        for j in range(UNROLL):
            i = m * UNROLL + j
            ex, ey, ez = [field[i, comp, low:high] for comp in range(3)]
            ey_up, ez_up = [field[i + 1, comp, low:high] for comp in (1, 2)]
            ex_next, ez_next = [field[i, comp, low + 1 : high + 1] for comp in (0, 2)]
            nu = rel[i, low:high]
            hx = nu * ((ez_next - ez) - (next_z(ey) - ey))
            hy = nu * ((next_z(ex) - ex) - (ez_up - ez))
            hz = nu * ((ey_up - ey) - (ex_next - ex))
            kx = crop(prev_z(hy) - hy) - crop(prev_y_in(hz) - hz)
            ky = crop(hz_low - hz) - crop(prev_z(hx) - hx)
            kz = crop(prev_y_in(hx) - hx) - crop(hy_low - hy)
            emit(i, rows, (kx, ky, kz))
            hy_low, hz_low = hy, hz
        return hy_low, hz_low

    zero = jnp.zeros((count, 128), jnp.float32)
    lax.fori_loop(0, planes // UNROLL, body, (zero, zero))


def load_rows(dst, other, low, own, high, blocks):
    zero = jnp.zeros((ROWS, 128), jnp.float32)
    edge = low.shape[3]

    def body(b, _):
        for j in range(2):
            for comp in range(3):
                i = 2 * b + j
                if edge < ROWS:
                    dst[i, comp, 0:ROWS] = zero
                    dst[i, comp, 2 * ROWS : 3 * ROWS] = zero
                dst[i, comp, ROWS - edge : ROWS] = low[b, comp, j]
                dst[i, comp, ROWS : 2 * ROWS] = own[b, comp, j]
                dst[i, comp, 2 * ROWS : 2 * ROWS + edge] = high[b, comp, j]
                dst[i, comp, 3 * ROWS : 4 * ROWS] = zero
                other[i, comp, 3 * ROWS : 4 * ROWS] = zero
        return 0

    lax.fori_loop(0, blocks, body, 0)
    for comp in range(3):
        dst[2 * blocks, comp] = jnp.zeros((4 * ROWS, 128), jnp.float32)
        other[2 * blocks, comp] = jnp.zeros((4 * ROWS, 128), jnp.float32)


MID = pl.ds(ROWS, ROWS)


def fine_kernel(first, flags, low, own, high, con, rel, *rest):
    if first:
        total, after, here, there, quot, nu2 = rest
    else:
        other, base, out, total, here, there, quot, nu2 = rest
    blocks = own.shape[0]
    planes = 2 * blocks
    theta, delta, weights, scale = FINE
    load_rows(here, there, low, own, high, blocks)

    def prepare(i, _):
        quot[i] = 2.0 * theta / delta - (2.0 * FSTEPS / delta) * con[i]
        nu2[i] = (2.0 / delta) * rel[i]
        return 0

    lax.fori_loop(0, planes, prepare, 0)

    buffers = (here, there)
    sweeps = FSWEEPS if first else FSWEEPS - 1
    for k in range(sweeps):
        now, new = buffers[k % 2], buffers[(k + 1) % 2]

        def emit(i, rows, curl, k=k, now=now, new=new):
            b, j = i // 2, i % 2
            q = quot[i, rows]
            for comp in range(3):
                v = q * now[i, comp, rows] - curl[comp]
                v = 0.5 * v if k == 0 else v - new[i, comp, rows]
                acc = weights[k] * now[i, comp, MID]
                if k > 0:
                    acc = total[b, comp, j] + acc
                elif not first:
                    acc = other[b, comp, j] + acc
                if k + 1 < sweeps:
                    new[i, comp, rows] = v
                elif first:
                    after[b, comp, j] = (1.0 / scale) * v + (FSTEPS * con[i, MID]) * acc
                else:
                    acc = acc + weights[k + 1] * v
                    out[b, comp, j] = base[b, comp, j] + acc
                total[b, comp, j] = acc

        curl_sweep(now, nu2, flags[0], sweeps - 1 - k, emit, planes)


def coarse_kernel(count, gate, flags, low, own, high, con, rel, *rest):
    if gate is None:
        out, state, curled, fac, nu3 = rest
    else:
        extra, out, state, curled, fac, nu3 = rest
    blocks = own.shape[0]
    planes = 2 * blocks
    theta, delta, weights, _ = COARSE
    load_rows(state, curled, low, own, high, blocks)

    def prepare(i, _):
        fac[i] = (weights[0] + weights[1] * theta / delta) - (weights[1] / delta) * con[i]
        nu3[i] = (weights[1] / delta) * rel[i]
        return 0

    lax.fori_loop(0, planes, prepare, 0)

    for n in range(count):
        margin = 2 * (count - 1 - n)

        def first(i, rows, curl):
            for comp in range(3):
                curled[i, comp, rows] = curl[comp]

        curl_sweep(state, rel, flags[0], margin + 1, first, planes)

        def second(i, rows, curl, margin=margin):
            f = fac[i, rows]
            for comp in range(3):
                v = state[i, comp, rows] - f * curled[i, comp, rows] + curl[comp]
                if margin:
                    state[i, comp, rows] = v
                elif gate is None:
                    out[i // 2, comp, i % 2] = v
                else:
                    out[i // 2, comp, i % 2] = extra[i // 2, comp, i % 2] + jnp.where(flags[gate] > 0.0, v, 0.0)

        curl_sweep(curled, nu3, flags[0], margin, second, planes)


def plane_curls(ny):
    next_z, prev_z, raw_next, raw_prev = shifts((ny, 128))
    row = lax.broadcasted_iota(jnp.int32, (ny, 128), 0)

    def next_y(v):
        return jnp.where(row < ny - 1, raw_next(v), 0.0)

    def prev_y(v):
        return jnp.where(row > 0, raw_prev(v), 0.0)

    def curl(nu, e, up):
        ex, ey, ez = e
        hx = nu * ((next_y(ez) - ez) - (next_z(ey) - ey))
        hy = nu * ((next_z(ex) - ex) - (up[1] - ez))
        hz = nu * ((up[0] - ey) - (next_y(ex) - ex))
        return hx, hy, hz

    def back(h, low):
        hx, hy, hz = h
        kx = (prev_z(hy) - hy) - (prev_y(hz) - hz)
        ky = (low[2] - hz) - (prev_z(hx) - hx)
        kz = (prev_y(hx) - hx) - (low[1] - hy)
        return kx, ky, kz

    return curl, back


def spread(ref, comp, i, v):
    for b in range(v.shape[0] // ROWS):
        ref[b, comp, i] = v[b * ROWS : (b + 1) * ROWS]


def residual_kernel(flags, state, src, rel, up, low, rel_low, res):
    planes, ny = rel.shape[0], rel.shape[1]
    curl, back = plane_curls(ny)
    before = curl(rel_low[0], (low[0], low[1], low[2]), (state[1, 0], state[2, 0]))
    for i in range(planes):
        nxt = (state[1, i + 1], state[2, i + 1]) if i + 1 < planes else (up[0], up[1])
        here = curl(rel[i], (state[0, i], state[1, i], state[2, i]), nxt)
        k = back(here, before)
        for comp in range(3):
            spread(res, comp, i, src[comp, i] - k[comp])
        before = here


def base_kernel(flags, state, old, src, con, rel, up, low, rel_low, begin, begin_up, begin_low, base, work):
    planes, ny = con.shape[0], con.shape[1]
    theta, delta, weights, _ = COARSE
    curl, back = plane_curls(ny)

    def fac(i):
        return (weights[0] + weights[1] * theta / delta) - (weights[1] / delta) * con[i]

    before = curl(rel_low[0], (low[0], low[1], low[2]), (src[1, 0], src[2, 0]))
    for i in range(planes):
        nxt = (src[1, i + 1], src[2, i + 1]) if i + 1 < planes else (up[0], up[1])
        here = curl(rel[i], (src[0, i], src[1, i], src[2, i]), nxt)
        k = back(here, before)
        for comp in range(3):
            push = fac(i) * src[comp, i] - (weights[1] / delta) * k[comp]
            spread(base, comp, i, state[comp, i] - old[comp, i] + push)
        before = here

    @pl.when(flags[1] > 0.0)
    def _():
        def part(i, comp):
            if i < 0:
                return begin_low[comp * planes + planes + i]
            return begin[comp, i] if i < planes else begin_up[comp * planes + i - planes]

        def nu(i):
            if i < 0:
                return begin_low[3 * planes + planes + i]
            return rel[i] if i < planes else begin_up[3 * planes + i - planes]

        def h_of(i):
            above = (part(i + 1, 1), part(i + 1, 2))
            return curl(nu(i), (part(i, 0), part(i, 1), part(i, 2)), above)

        before = h_of(-2)
        for i in range(-1, planes + 1):
            here = h_of(i)
            k = back(here, before)
            for comp in range(3):
                work[i + 1, comp] = k[comp] * flags[2] if i == planes else k[comp]
            before = here
        before = None
        for i in range(-1, planes):
            u = [work[i + 1, comp] for comp in range(3)]
            here = curl(nu(i), u, (work[i + 2, 1], work[i + 2, 2]))
            if i >= 0:
                k = back(here, before)
                for comp in range(3):
                    v = begin[comp, i] - fac(i) * u[comp] + (weights[1] / delta) * k[comp]
                    for b in range(ny // ROWS):
                        base[b, comp, i] = base[b, comp, i] + v[b * ROWS : (b + 1) * ROWS]
            before = here


VMEM = pl.BlockSpec(memory_space=pltpu.VMEM)
SMEM = pl.BlockSpec(memory_space=pltpu.SMEM)


def call(kernel, outs, scratch, flags, *operands):
    return pl.pallas_call(
        kernel,
        out_shape=[jax.ShapeDtypeStruct(s, jnp.float32) for s in outs],
        in_specs=[SMEM] + [VMEM] * len(operands),
        out_specs=[VMEM] * len(outs),
        scratch_shapes=[pltpu.VMEM(s, jnp.float32) for s in scratch],
        compiler_params=pltpu.CompilerParams(vmem_limit_bytes=VMEM_LIMIT),
    )(flags, *operands)


def open_shift(value, steps):
    count = lax.axis_size("space")
    first, last = max(0, -steps), min(count, count - steps)
    return lax.ppermute(value, "space", [(i, i + steps) for i in range(first, last)])


def ring_shift(value, steps):
    count = lax.axis_size("slab")
    return lax.ppermute(value, "slab", [(i, (i + steps) % count) for i in range(count)])


def both_shift(value, steps, along):
    slabs, spaces = lax.axis_size("slab"), lax.axis_size("space")
    pairs = [
        (i * spaces + k, (i + steps) % slabs * spaces + k + along)
        for i in range(slabs)
        for k in range(spaces)
        if 0 <= k + along < spaces
    ]
    return lax.ppermute(value, ("slab", "space"), pairs)


def turn(value):
    return lax.all_to_all(value, "space", 0, 0, tiled=True)


def halo(value):
    return open_shift(value, 1), open_shift(value, -1)


def step(state_old, coarse_old, source, start_state, conduct, reluct, converged):
    groups = lax.axis_size("slab")
    spaces = lax.axis_size("space")
    position = (lax.axis_index("slab") - converged[0] % groups - 1) % groups
    inner = lax.axis_index("space") < spaces - 1
    flags = jnp.stack((inner, position == 0, inner, position >= 1, position >= 2)).astype(jnp.float32)
    state, old, src = state_old[0], coarse_old[0], source[0]
    planes, ny = conduct.shape[0], conduct.shape[1]
    blocks = spaces
    nx = blocks * planes
    field = (blocks, 3, planes, ROWS, 128)

    ups = open_shift(jnp.stack((state[1:3, 0], src[1:3, 0])), -1)
    lows = open_shift(jnp.concatenate((state[:, -1], src[:, -1], reluct[-1:])), 1)
    coef = jnp.stack((conduct, reluct)).reshape(2, planes, blocks, ROWS, 128).transpose(2, 0, 1, 3, 4)
    coef = turn(coef)
    coef_low, coef_high = halo(coef)
    coef24 = jnp.concatenate((coef_low, coef, coef_high), 3).transpose(1, 0, 2, 3, 4).reshape(2, nx, 3 * ROWS, 128)
    con, rel = coef24[0], coef24[1]

    (res,) = call(residual_kernel, [field], [], flags, state, src, reluct, ups[0], lows[0:3], lows[6:7])
    res = turn(res)
    res_low, res_high = halo(res)

    start_state, res = lax.optimization_barrier((start_state, res))
    edge = jnp.concatenate((start_state.reshape(3 * planes, ny, 128), reluct))
    edge_low, edge_high = halo(edge)

    wide = (nx + 1, 3, 4 * ROWS, 128)
    slim = (nx, 3 * ROWS, 128)
    scratch = [wide, wide, slim, slim]
    total, after = call(
        functools.partial(fine_kernel, True), [field, field], scratch, flags,
        res_low, res, res_high, con, rel,
    )
    after_low, after_high = halo(after)
    src, after = lax.optimization_barrier((src, after))
    (base,) = call(
        base_kernel, [field], [(planes + 2, 3, ny, 128)], flags,
        state, old, src, conduct, reluct, ups[1], lows[3:6], lows[6:7], start_state, edge_high, edge_low,
    )
    base = turn(base)

    lead, total = call(
        functools.partial(fine_kernel, False), [field, field], scratch, flags,
        after_low, after, after_high, con, rel, total, base,
    )

    def coarse(value, count):
        low, high = halo(value)
        return call(
            functools.partial(coarse_kernel, count, None), [field], scratch, flags,
            low, value, high, con, rel,
        )[0]

    def joined(value, steps, gate):
        rows = 2 * steps
        own = ring_shift(value, steps)
        low = both_shift(value[:, :, :, ROWS - rows :], steps, 1)
        high = both_shift(value[:, :, :, :rows], steps, -1)
        return call(
            functools.partial(coarse_kernel, steps, gate), [field], scratch, flags,
            low, own, high, con, rel, value,
        )[0]

    lead = joined(lead, 1, 3)
    total, lead = lax.optimization_barrier((total, lead))
    total = turn(total)
    lead = joined(lead, 2, 4)
    final, power = lead, lead
    for steps in range(4, groups, 4):
        power = coarse(power, 4)
        moved = ring_shift(power, steps)
        final = final + jnp.where(position >= steps, moved, 0.0)

    def home(value):
        return value.transpose(1, 2, 0, 3, 4).reshape(3, planes, ny, 128)

    turned = turn(final)
    starts = ring_shift(turned, 1)
    coarse_new = (home(turned) - home(total)) + (old - state)
    state_new = jnp.where(position == 0, start_state, home(starts))
    return state_new[None], coarse_new[None]


def solution(mesh):
    placed = (
        P("slab", None, "space", None, None),
        P("slab", None, "space", None, None),
        P("slab", None, "space", None, None),
        P(None, "space", None, None),
        P("space", None, None),
        P("space", None, None),
        P(),
    )
    return jax.shard_map(
        step,
        mesh=mesh,
        in_specs=placed,
        out_specs=(P("slab", None, "space", None, None), P("slab", None, "space", None, None)),
        check_vma=False,
    )
```
